256 devices in a mesh: area: 32 (over z, y_lo, core), win: 8 (over y_hi, x).
Axes of the slice: x: 4, y: 4 (y_hi: 2, y_lo: 2; y = y_hi * 2 + y_lo), z: 8, core: 2. Of those that a mesh axis runs over, the one named last changes fastest.
Arguments:
- kkt: bfloat16 [32, 8, 1536, 1536], P('area', 'win'), as said below
- offsets: float32 [32, 8, 1536, 256], P('area', 'win'), may hold values from -6 to 6
- lower: float32 [32, 8, 1536], P('area', 'win'), may hold values from -1.2 to -0.4
- upper: float32 [32, 8, 1536], P('area', 'win'), may hold values from 0.4 to 1.2
- partners: int32 [4, 32], replicated, may hold values from 0 to 31, as said below
- adjacency: int32 [32, 32], replicated, may hold values from 0 to 1, as said below
Outputs:
- consensus: float32 [32, 8, 1536, 256], P('area', 'win')
- duals: float32 [32, 8, 1536, 256], P('area', 'win')
The draws below stay inside these ranges and needn't reach their ends.
Inputs may be any that keep to these rules, and one draw needn't show every extreme that they name: `partners`: row k is the perfect matching a -> a XOR c_k for a colour c_k between 1 and 31. `adjacency`: symmetric with a zero diagonal. `kkt`: each block is a dense full-rank matrix with a positive diagonal.
All inputs are finite; a program needn't handle non-finite values.
Results may differ from the reference program's by a relative error of at most 0.0028.
Values sent between devices are 32-bit elements; how exact they have to be, the bound alone decides.
No kernel may reach another device: no remote copies, remote signals or barrier semaphores. Data moves between devices by JAX's collectives and lax.ppermute only.
A program may use at most 64 MiB of HBM per device.

```python
import jax
import jax.numpy as jnp
from jax import lax

K = 1536
COUPLE = 512
BOUND = 256
S = 256
ITERS = 4
N_AREA = 32
N_WIN = 8


def draw_kkt(key, part):
    key_off = jax.random.fold_in(key, 11)
    key_diag = jax.random.fold_in(key, 12)
    off = jax.random.normal(key_off, (N_AREA, N_WIN, K, K), jnp.float32) * 0.4 / jnp.sqrt(1.0 * K)
    diag = jnp.exp(jax.random.uniform(key_diag, (N_AREA, N_WIN, K, 1), jnp.float32, jnp.log(0.4), jnp.log(1.2)))
    eye = jnp.eye(K, dtype=jnp.float32)
    return (off + eye[None, None] * diag).astype(jnp.bfloat16)


def draw_partners(key, part):
    colours = jax.random.randint(jax.random.fold_in(key, 21), (ITERS,), 1, N_AREA)
    areas = jnp.arange(N_AREA, dtype=jnp.int32)
    return jnp.bitwise_xor(areas[None, :], colours[:, None]).astype(jnp.int32)


def draw_adjacency(key, part):
    bits = jax.random.randint(jax.random.fold_in(key, 31), (N_AREA, N_AREA), 0, 2)
    upper_part = jnp.triu(bits, 1)
    return (upper_part + upper_part.T).astype(jnp.int32)


def steps_of(own_key, extent, cuts, least, top_value):
    level, own = 1.0, jax.random.fold_in(own_key, 6)
    for axis_at, parts in cuts:
        heights = jnp.exp(jax.random.uniform(jax.random.fold_in(own, axis_at), (parts,), jnp.float32, least / len(cuts), top_value / len(cuts)))
        level = level * jnp.repeat(heights, extent[axis_at] // parts).reshape([-1 if axis == axis_at else 1 for axis in range(len(extent))])
    return level


def normal_values(rng, dims, scale, limit, split=(), kind=jnp.bfloat16):
    entries = jax.random.normal(rng, dims, jnp.float32) * scale
    if len(split) > 0:
        entries = steps_of(rng, dims, split, -0.22, 0.18) * entries
    return jnp.clip(entries, min=-limit, max=limit).astype(kind)


def setup_inputs(seed: int = 0) -> dict:
    streams_of = jax.random.split(jax.random.key(seed), 7)
    return {
        "kkt": draw_kkt(jax.random.fold_in(streams_of[6], 71), 0),
        "offsets": normal_values(streams_of[1], (N_AREA, N_WIN, K, S), 1.0, 6.0, ((0, 32), (1, 8)), jnp.float32),
        "lower": jnp.clip(-1.2 + 0.800000042 * jax.random.uniform(streams_of[2], (N_AREA, N_WIN, K), jnp.float32) ** steps_of(streams_of[2], (N_AREA, N_WIN, K), ((0, 32), (1, 8)), -0.2, 0.2), -1.2, -0.4),
        "upper": jnp.clip(0.4 + 0.800000042 * jax.random.uniform(streams_of[3], (N_AREA, N_WIN, K), jnp.float32) ** steps_of(streams_of[3], (N_AREA, N_WIN, K), ((0, 32), (1, 8)), -0.2, 0.2), 0.4, 1.2),
        "partners": draw_partners(jax.random.fold_in(streams_of[6], 71), 0),
        "adjacency": draw_adjacency(jax.random.fold_in(streams_of[6], 71), 0),
    }


def apply_block(pair):
    return jnp.dot(pair[0], pair[1], preferred_element_type=jnp.float32)


def reference(kkt, offsets, lower, upper, partners, adjacency):
    z_now = jnp.zeros_like(offsets)
    u_now = jnp.zeros_like(offsets)
    low = lower[..., None]
    high = upper[..., None]
    areas = jnp.arange(N_AREA).astype(jnp.int32)
    flat_kkt = kkt.reshape(N_AREA * N_WIN, K, K)
    for step in range(ITERS):
        v_now = (offsets + z_now - u_now).astype(jnp.bfloat16)
        x_now = lax.map(apply_block, (flat_kkt, v_now.reshape(N_AREA * N_WIN, K, S)))
        x_now = x_now.reshape(N_AREA, N_WIN, K, S)
        y_now = jnp.minimum(jnp.maximum(x_now + u_now, low), high)
        row = partners[step]
        couple = y_now[:, :, :COUPLE]
        other = couple[row]
        linked = (adjacency[areas, row] == 1).astype(offsets.dtype)[:, None, None, None]
        new_couple = couple + linked * 0.5 * (other - couple)
        ends = y_now[:, :, COUPLE:COUPLE + BOUND]
        before = jnp.concatenate([jnp.zeros_like(ends[:, :1]), ends[:, :-1]], axis=1)
        starts = 0.5 * (y_now[:, :, COUPLE + BOUND:COUPLE + 2 * BOUND] + before)
        z_now = jnp.concatenate([new_couple, ends, starts, y_now[:, :, COUPLE + 2 * BOUND:]], axis=2)
        u_now = u_now + x_now - z_now
    return z_now, u_now
```

```python
import jax
import jax.numpy as jnp
from jax import lax
from jax.sharding import PartitionSpec as P

COUPLE = 512
BOUND = 256
ITERS = 4


def from_behind(array, axis, by):
    length = lax.axis_size(axis)
    pairs = [(i, i + by) for i in range(length) if 0 <= i + by < length]
    return lax.ppermute(array, axis, pairs)


def exchange(array, colour, axis):
    length = lax.axis_size(axis)

    def swap(bits):
        pairs = [(i, i ^ bits) for i in range(length)]
        return lambda block: lax.ppermute(block, axis, pairs)

    return lax.switch(colour - 1, [swap(bits) for bits in range(1, length)], array)


def local(kkt, offsets, lower, upper, partners, adjacency):
    matrix = kkt[0, 0]
    costs = offsets[0, 0]
    low = lower[0, 0][:, None]
    high = upper[0, 0][:, None]
    sent = COUPLE + BOUND
    area = lax.axis_index("area")

    def iterate(step, carry):
        z_now, u_now = carry
        v_now = (costs + z_now - u_now).astype(jnp.bfloat16)
        x_head = jnp.dot(matrix[:sent], v_now, preferred_element_type=jnp.float32)
        y_head = jnp.minimum(jnp.maximum(x_head + u_now[:sent], low[:sent]), high[:sent])
        couple = y_head[:COUPLE]
        ends = y_head[COUPLE:sent]
        before = from_behind(ends, "win", 1)
        row = partners[step]
        other = exchange(couple, row[0], "area")
        linked = (adjacency[area, row[area]] == 1).astype(couple.dtype)
        new_couple = couple + linked * 0.5 * (other - couple)
        x_tail = jnp.dot(matrix[sent:], v_now, preferred_element_type=jnp.float32)
        y_tail = jnp.minimum(jnp.maximum(x_tail + u_now[sent:], low[sent:]), high[sent:])
        starts = 0.5 * (y_tail[:BOUND] + before)
        z_next = jnp.concatenate([new_couple, ends, starts, y_tail[BOUND:]], axis=0)
        x_full = jnp.concatenate([x_head, x_tail], axis=0)
        return z_next, u_now + x_full - z_next

    z_now, u_now = lax.fori_loop(0, ITERS, iterate, (jnp.zeros_like(costs), jnp.zeros_like(costs)))
    return (z_now[None, None], u_now[None, None])


def solution(mesh):
    in_specs = (
        P("area", "win", None, None),
        P("area", "win", None, None),
        P("area", "win", None),
        P("area", "win", None),
        P(),
        P(),
    )
    out_specs = (P("area", "win", None, None), P("area", "win", None, None))
    return jax.shard_map(local, mesh=mesh, in_specs=in_specs, out_specs=out_specs, check_vma=False)
```

```python
import jax
import jax.numpy as jnp
from jax import lax
from jax.experimental import pallas as pl
from jax.experimental.pallas import tpu as pltpu
from jax.sharding import PartitionSpec as P

COUPLE = 512
BOUND = 256
SENT = COUPLE + BOUND
ITERS = 4
ROWS = 256
LANES = 128
BITS = 5

ANY = pl.BlockSpec(memory_space=pltpu.HBM)
VMEM = pl.BlockSpec(memory_space=pltpu.VMEM)
SMEM = pl.BlockSpec(memory_space=pltpu.SMEM)


def f32(*shape):
    return jax.ShapeDtypeStruct(shape, jnp.float32)


def transfers(couple, ends, colour):
    areas = lax.axis_size("area")
    windows = lax.axis_size("win")
    onward = [(i, i + 1) for i in range(windows - 1)]

    def swap(bits):
        pairs = [(i, i ^ bits) for i in range(areas)]
        return lambda c, e: (lax.ppermute(c, "area", pairs), lax.ppermute(e, "win", onward))

    return lax.switch(colour - 1, [swap(bits) for bits in range(1, areas)], couple, ends)


def clip(total, low, high):
    width = total.shape[1] // LANES
    low, high = (jnp.concatenate([b] * width, axis=1) for b in (low, high))
    return jnp.minimum(jnp.maximum(total, low), high)


def prepare_kernel(area, partners, adjacency, lower, upper, halves, code, low, high, *unset):
    packed = 0
    for k in range(ITERS):
        mate = partners[k, area[0]]
        halves[k] = jnp.where(adjacency[area[0], mate] == 1, 0.5, 0.0)
        packed = packed + (partners[k, 0] << (BITS * k))
    code[0] = packed
    for source, target in ((lower, low), (upper, high)):
        for start in range(0, source.shape[1], LANES):
            line = source[0:1, start : start + LANES]
            target[start : start + LANES, :] = jnp.broadcast_to(line, (LANES, LANES)).T


def prepare(area, partners, adjacency, lower, upper, width):
    size = lower.shape[1]
    return pl.pallas_call(
        prepare_kernel,
        out_shape=(f32(ITERS), jax.ShapeDtypeStruct((1,), jnp.int32), f32(size, LANES), f32(size, LANES),
                   f32(size, width), f32(COUPLE, width), f32(BOUND, width)),
        in_specs=[SMEM, SMEM, SMEM, VMEM, VMEM],
        out_specs=(SMEM, SMEM, VMEM, VMEM, ANY, ANY, ANY),
        name="prepare",
    )(area, partners, adjacency, lower, upper)


def step_kernel(
    step_ref, halves, matrix_hbm, low_hbm, high_hbm, costs, total, other, before,
    total_out, couple, ends, matrix, low, high, v_ref, sems,
):
    size, width = total.shape
    blocks = size // ROWS
    at = lambda block: pl.ds(block * ROWS, ROWS)
    copies = lambda pairs, sem: [pltpu.make_async_copy(a, b, sem) for a, b in pairs]
    bounds = [copies([(low_hbm.at[at(i), :], low.at[at(i), :])], sems.at[0, i])
              + copies([(high_hbm.at[at(i), :], high.at[at(i), :])], sems.at[1, i]) for i in range(blocks)]
    rows_of = [copies([(matrix_hbm.at[at(i), :], matrix.at[at(i), :])], sems.at[2, i]) for i in range(blocks)]
    for group in bounds + rows_of:
        for copy in group:
            copy.start()
    now = step_ref[0]

    @pl.when(now == 0)
    def _():
        v_ref[...] = costs[...].astype(jnp.bfloat16)
        total_out[...] = jnp.zeros_like(total_out)
        for group in bounds:
            for copy in group:
                copy.wait()

    @pl.when(now > 0)
    def _():
        half = halves[jnp.maximum(now - 1, 0)]
        for i in range(blocks):
            for copy in bounds[i]:
                copy.wait()
            rows = slice(i * ROWS, (i + 1) * ROWS)
            t = total[rows, :]
            z = clip(t, low[rows, :], high[rows, :])
            if i < COUPLE // ROWS:
                z = z + half * (other[rows, :] - z)
            elif i == SENT // ROWS:
                z = 0.5 * (z + before[...])
            u = t - z
            v_ref[rows, :] = (costs[rows, :] + z - u).astype(jnp.bfloat16)
            total_out[rows, :] = u

    for i in range(blocks):
        for copy in rows_of[i]:
            copy.wait()
        rows = slice(i * ROWS, (i + 1) * ROWS)
        x = jnp.dot(matrix[rows, :], v_ref[...], preferred_element_type=jnp.float32)
        t = total_out[rows, :] + x
        total_out[rows, :] = t
        if i < COUPLE // ROWS:
            couple[rows, :] = clip(t, low[rows, :], high[rows, :])
        elif i < SENT // ROWS:
            ends[...] = clip(t, low[rows, :], high[rows, :])


def step(index, halves, matrix, low, high, costs, total, other, before):
    size, width = total.shape
    return pl.pallas_call(
        step_kernel,
        out_shape=(f32(size, width), f32(COUPLE, width), f32(BOUND, width)),
        in_specs=[SMEM, SMEM, ANY, ANY, ANY] + [VMEM] * 4,
        out_specs=(VMEM, VMEM, VMEM),
        input_output_aliases={6: 0},
        scratch_shapes=[
            pltpu.VMEM(matrix.shape, matrix.dtype),
            pltpu.VMEM(low.shape, jnp.float32),
            pltpu.VMEM(high.shape, jnp.float32),
            pltpu.VMEM((size, width), jnp.bfloat16),
            pltpu.SemaphoreType.DMA((3, size // ROWS)),
        ],
        compiler_params=pltpu.CompilerParams(vmem_limit_bytes=32 * 1024 * 1024),
        cost_estimate=pl.CostEstimate(
            flops=2 * size * size * width, bytes_accessed=2 * size * size + 20 * size * width, transcendentals=0
        ),
        name="step",
    )(index, halves, matrix, low, high, costs, total, other, before)


def finish_kernel(halves, low, high, total, other, before, z_out, u_out):
    half = halves[ITERS - 1]
    t = total[...]
    block = pl.program_id(0)
    y = clip(t, low[...], high[...])

    def put(z):
        z_out[...] = z
        u_out[...] = t - z

    @pl.when(block < COUPLE // ROWS)
    def _():
        put(y + half * (other[...] - y))

    @pl.when(block == SENT // ROWS)
    def _():
        put(0.5 * (y + before[...]))

    @pl.when((block >= COUPLE // ROWS) & (block != SENT // ROWS))
    def _():
        put(y)


def finish(halves, low, high, total, other, before):
    size, width = total.shape
    full = pl.BlockSpec((ROWS, width), lambda i: (i, 0))
    bound = pl.BlockSpec((ROWS, LANES), lambda i: (i, 0))
    return pl.pallas_call(
        finish_kernel,
        out_shape=(f32(size, width), f32(size, width)),
        grid=(size // ROWS,),
        in_specs=[
            SMEM,
            bound,
            bound,
            full,
            pl.BlockSpec((ROWS, width), lambda i: (jnp.minimum(i, COUPLE // ROWS - 1), 0)),
            pl.BlockSpec((ROWS, width), lambda i: (0, 0)),
        ],
        out_specs=(full, full),
        name="finish",
    )(halves, low, high, total, other, before)


def local(kkt, offsets, lower, upper, partners, adjacency):
    matrix = kkt[0, 0]
    costs = offsets[0, 0]
    area = lax.axis_index("area")[None].astype(jnp.int32)
    halves, code, low, high, total, other, before = prepare(
        area, partners, adjacency, lower[0], upper[0], costs.shape[1]
    )

    def iterate(k, carry):
        code, total, other, before = carry
        total, couple, ends = step(k[None], halves, matrix, low, high, costs, total, other, before)
        other, before = transfers(couple, ends, code & (2**BITS - 1))
        return code >> BITS, total, other, before

    _, total, other, before = lax.fori_loop(0, ITERS, iterate, (code[0], total, other, before))
    z_now, u_now = finish(halves, low, high, total, other, before)
    return (z_now[None, None], u_now[None, None])


def solution(mesh):
    in_specs = (
        P("area", "win", None, None),
        P("area", "win", None, None),
        P("area", "win", None),
        P("area", "win", None),
        P(),
        P(),
    )
    out_specs = (P("area", "win", None, None), P("area", "win", None, None))
    return jax.shard_map(local, mesh=mesh, in_specs=in_specs, out_specs=out_specs, check_vma=False)
```

```python
import jax
import jax.numpy as jnp
from jax import lax
from jax.experimental import pallas as pl
from jax.experimental.pallas import tpu as pltpu
from jax.sharding import PartitionSpec as P

COUPLE = 512
BOUND = 256
HEAD = COUPLE + BOUND
ITERS = 4
ROWS = 256
LANES = 128
BITS = 5
CHUNK = 64

HBM = pl.BlockSpec(memory_space=pltpu.HBM)
VMEM = pl.BlockSpec(memory_space=pltpu.VMEM)
SMEM = pl.BlockSpec(memory_space=pltpu.SMEM)


def f32(*shape):
    return jax.ShapeDtypeStruct(shape, jnp.float32)


def bf16(*shape):
    return jax.ShapeDtypeStruct(shape, jnp.bfloat16)


def clip(total, low, high):
    width = total.shape[1] // LANES
    low, high = (jnp.concatenate([b] * width, axis=1) for b in (low, high))
    return jnp.minimum(jnp.maximum(total, low), high)


def product(left, right):
    return jnp.dot(left, right, preferred_element_type=jnp.float32)


def prepare_kernel(
    area, partners, adjacency, lower, upper, matrix_hbm, costs_hbm,
    code, low, high, v_own, partial, *rest,
):
    *_, matrix, costs, sems = rest
    end, other = pl.ds(COUPLE, BOUND), pl.ds(HEAD + BOUND, costs_hbm.shape[0] - HEAD - BOUND)
    own = (pl.ds(0, BOUND), pl.ds(BOUND, costs_hbm.shape[0] - HEAD - BOUND))
    move = pltpu.make_async_copy
    copies = [
        move(costs_hbm.at[end, :], costs.at[own[0], :], sems.at[0]),
        move(costs_hbm.at[other, :], costs.at[own[1], :], sems.at[1]),
        move(matrix_hbm.at[pl.ds(0, HEAD), end], matrix.at[:, own[0]], sems.at[2]),
        move(matrix_hbm.at[pl.ds(0, HEAD), other], matrix.at[:, own[1]], sems.at[3]),
    ]
    for copy in copies:
        copy.start()
    packed = 1 << (BITS * (ITERS + 1))
    for k in range(ITERS):
        linked = adjacency[area[0], partners[k, area[0]]] == 1
        packed = packed + (jnp.where(linked, partners[k, 0], 0) << (BITS * (k + 1)))
    code[0] = packed
    for source, target in ((lower, low), (upper, high)):
        for start in range(0, source.shape[1], LANES):
            line = source[0:1, start : start + LANES]
            target[start : start + LANES, :] = jnp.broadcast_to(line, (LANES, LANES)).T
    for copy in copies:
        copy.wait()
    v_own[...] = costs[...].astype(jnp.bfloat16)

    @pl.loop(0, HEAD // ROWS)
    def _(i):
        rows = pl.ds(pl.multiple_of(i * ROWS, ROWS), ROWS)
        partial[rows, :] = product(matrix[rows, :], v_own[...])


def prepare(area, partners, adjacency, lower, upper, matrix, costs):
    size, width = costs.shape
    rest = size - HEAD
    return pl.pallas_call(
        prepare_kernel,
        out_shape=(jax.ShapeDtypeStruct((1,), jnp.int32), f32(size, LANES), f32(size, LANES),
                   bf16(rest, width), f32(HEAD, width),
                   f32(HEAD, width), f32(rest, width), f32(COUPLE, width), f32(BOUND, width)),
        in_specs=[SMEM, SMEM, SMEM, VMEM, VMEM, HBM, HBM],
        out_specs=(SMEM, VMEM, VMEM, VMEM, VMEM, HBM, HBM, HBM, HBM),
        scratch_shapes=[
            pltpu.VMEM((HEAD, rest), matrix.dtype),
            pltpu.VMEM((rest, width), jnp.float32),
            pltpu.SemaphoreType.DMA((4,)),
        ],
        name="prepare",
    )(area, partners, adjacency, lower, upper, matrix, costs)


def lead_kernel(
    code, matrix_hbm, costs_hbm, low, high, head_hbm, tail_hbm, v_own_hbm, partial_hbm, other_hbm, before_hbm,
    head_out, couple, ends, v_full, rest,
    head, start, matrix, matrix_start, costs, partial, other, before, sems,
):
    move = pltpu.make_async_copy
    couples, starts = pl.ds(0, COUPLE), pl.ds(HEAD, BOUND)
    first = [
        move(head_hbm.at[couples, :], head, sems.at[0]),
        move(other_hbm, other, sems.at[1]),
        move(costs_hbm.at[couples, :], costs.at[couples, :], sems.at[2]),
    ]
    second = [
        move(tail_hbm.at[pl.ds(0, BOUND), :], start, sems.at[3]),
        move(before_hbm, before, sems.at[4]),
        move(costs_hbm.at[starts, :], costs.at[pl.ds(COUPLE, BOUND), :], sems.at[5]),
    ]
    third = [
        move(matrix_hbm.at[pl.ds(0, HEAD), couples], matrix, sems.at[6]),
        move(matrix_hbm.at[pl.ds(0, HEAD), starts], matrix_start, sems.at[7]),
        move(partial_hbm, partial, sems.at[8]),
    ]
    others = tail_hbm.shape[0] - BOUND
    last = [
        move(v_own_hbm.at[pl.ds(0, BOUND), :], v_full.at[pl.ds(COUPLE, BOUND), :], sems.at[9]),
        move(v_own_hbm.at[pl.ds(BOUND, others), :], v_full.at[pl.ds(HEAD + BOUND, others), :], sems.at[10]),
        move(tail_hbm.at[pl.ds(BOUND, others), :], rest.at[pl.ds(BOUND, others), :], sems.at[11]),
    ]
    for copy in first + second + third + last:
        copy.start()
    fresh = code[0] >= 1 << (BITS * (ITERS + 1))
    linked = (code[0] & (2**BITS - 1)) > 0
    for copy in first:
        copy.wait()

    @pl.when(fresh)
    def _():
        for copy in second:
            copy.wait()
        v_full[:COUPLE, :] = costs[:COUPLE, :].astype(jnp.bfloat16)
        v_full[HEAD : HEAD + BOUND, :] = costs[COUPLE:, :].astype(jnp.bfloat16)
        head_out[:COUPLE, :] = jnp.zeros((COUPLE, costs.shape[1]), jnp.float32)
        rest[:BOUND, :] = jnp.zeros((BOUND, costs.shape[1]), jnp.float32)

    @pl.when(jnp.logical_not(fresh))
    def _():
        for at in range(0, COUPLE, ROWS):
            rows = slice(at, at + ROWS)
            t = head[rows, :]
            y = clip(t, low[rows, :], high[rows, :])
            z = jnp.where(linked, y + 0.5 * (other[rows, :] - y), y)
            u = t - z
            v_full[rows, :] = (costs[rows, :] + z - u).astype(jnp.bfloat16)
            head_out[rows, :] = u
        for copy in second:
            copy.wait()
        rows = slice(HEAD, HEAD + BOUND)
        t = start[...]
        z = 0.5 * (clip(t, low[rows, :], high[rows, :]) + before[...])
        u = t - z
        v_full[rows, :] = (costs[COUPLE:, :] + z - u).astype(jnp.bfloat16)
        rest[:BOUND, :] = u

    for copy in third:
        copy.wait()
    for at in range(0, HEAD, ROWS):
        rows = slice(at, at + ROWS)
        x = product(matrix[rows, :], v_full[:COUPLE, :]) + product(matrix_start[rows, :], v_full[HEAD : HEAD + BOUND, :])
        t = partial[rows, :] + x
        if at < COUPLE:
            t = head_out[rows, :] + t
        head_out[rows, :] = t
        y = clip(t, low[rows, :], high[rows, :])
        if at < COUPLE:
            couple[rows, :] = y
        else:
            ends[...] = y
    for copy in last:
        copy.wait()

    @pl.when(fresh)
    def _():
        rest[BOUND:, :] = jnp.zeros((others, costs.shape[1]), jnp.float32)


def lead(code, matrix, costs, low, high, head, tail, v_own, partial, other, before):
    size, width = costs.shape
    return pl.pallas_call(
        lead_kernel,
        out_shape=(f32(HEAD, width), f32(COUPLE, width), f32(BOUND, width), bf16(size, width), f32(size - HEAD, width)),
        in_specs=[SMEM, HBM, HBM, VMEM, VMEM] + [HBM] * 6,
        out_specs=(VMEM,) * 5,
        input_output_aliases={5: 0},
        scratch_shapes=[
            pltpu.VMEM((COUPLE, width), jnp.float32),
            pltpu.VMEM((BOUND, width), jnp.float32),
            pltpu.VMEM((HEAD, COUPLE), matrix.dtype),
            pltpu.VMEM((HEAD, BOUND), matrix.dtype),
            pltpu.VMEM((HEAD, width), jnp.float32),
            pltpu.VMEM((HEAD, width), jnp.float32),
            pltpu.VMEM((COUPLE, width), jnp.float32),
            pltpu.VMEM((BOUND, width), jnp.float32),
            pltpu.SemaphoreType.DMA((12,)),
        ],
        compiler_params=pltpu.CompilerParams(vmem_limit_bytes=24 * 1024 * 1024),
        cost_estimate=pl.CostEstimate(
            flops=2 * HEAD * HEAD * width, bytes_accessed=2 * HEAD * HEAD + 30 * HEAD * width, transcendentals=0
        ),
        name="lead",
    )(code, matrix, costs, low, high, head, tail, v_own, partial, other, before)


def follow_kernel(
    matrix, costs_end, costs_rest, low, high, ends_total, v_full, rest,
    tail, v_own, partial, v_ref, total,
):
    step = pl.program_id(0)
    parts = tail.shape[0] // ROWS
    chunks = ROWS // CHUNK

    @pl.when(step == 0)
    def _():
        v_ref[...] = v_full[...]

    total[...] = jnp.zeros_like(total)
    first = step < parts

    @pl.loop(jnp.where(first, 0, 1), v_ref.shape[0] // COUPLE)
    def _(j):
        cut = pl.ds(pl.multiple_of(j * COUPLE, COUPLE), COUPLE)
        total[...] += product(matrix[:, cut], v_ref[cut, :])

    def bounded(t, at):
        return clip(t, low[at, :], high[at, :])

    @pl.when(step == 0)
    def _():
        tail[:BOUND, :] = rest[:BOUND, :] + total[...]

    @pl.when((step > 0) & first)
    def _():
        @pl.loop(0, chunks)
        def _(c):
            own = pl.ds(pl.multiple_of(c * CHUNK, CHUNK), CHUNK)
            rows = pl.ds(pl.multiple_of(step * ROWS + c * CHUNK, CHUNK), CHUNK)
            at = pl.ds(pl.multiple_of(HEAD + step * ROWS + c * CHUNK, CHUNK), CHUNK)
            cost = pl.ds(pl.multiple_of((step - 1) * ROWS + c * CHUNK, CHUNK), CHUNK)
            t = rest[rows, :]
            t = (t - bounded(t, at)) + total[own, :]
            tail[rows, :] = t
            y = bounded(t, at)
            v_own[rows, :] = (costs_rest[cost, :] + y - (t - y)).astype(jnp.bfloat16)

    @pl.when(step == parts - 1)
    def _():
        @pl.loop(0, chunks)
        def _(c):
            own = pl.ds(pl.multiple_of(c * CHUNK, CHUNK), CHUNK)
            at = pl.ds(pl.multiple_of(COUPLE + c * CHUNK, CHUNK), CHUNK)
            t = ends_total[own, :]
            y = bounded(t, at)
            v_own[own, :] = (costs_end[own, :] + y - (t - y)).astype(jnp.bfloat16)

        v_ref[COUPLE:HEAD, :] = v_own[:BOUND, :]
        v_ref[HEAD : HEAD + BOUND, :] = jnp.zeros((BOUND, v_ref.shape[1]), jnp.bfloat16)
        v_ref[HEAD + BOUND :, :] = v_own[BOUND:, :]

    @pl.when(step >= parts)
    def _():
        last = step == 2 * parts - 1

        @pl.loop(0, chunks)
        def _(c):
            own = pl.ds(pl.multiple_of(c * CHUNK, CHUNK), CHUNK)
            rows = pl.ds(pl.multiple_of((step - parts) * ROWS + c * CHUNK, CHUNK), CHUNK)
            at = pl.ds(pl.multiple_of(COUPLE + c * CHUNK, CHUNK), CHUNK)
            t = ends_total[own, :]
            u = t - bounded(t, at)
            partial[rows, :] = total[own, :] + jnp.where(last, u, 0.0)


def follow(matrix, costs, low, high, head, v_full, rest):
    size, width = costs.shape
    parts = (size - HEAD) // ROWS
    fixed = lambda rows, index: pl.BlockSpec((rows, width), lambda i: (index, 0))
    return pl.pallas_call(
        follow_kernel,
        grid=(2 * parts,),
        out_shape=(f32(*rest.shape), bf16(*rest.shape), f32(HEAD, width)),
        in_specs=[
            pl.BlockSpec((ROWS, size), lambda i: (jnp.where(i < parts, i + parts, i - parts), 0)),
            fixed(BOUND, COUPLE // BOUND),
            fixed(size - HEAD - BOUND, (HEAD + BOUND) // (size - HEAD - BOUND)),
            VMEM,
            VMEM,
            fixed(BOUND, COUPLE // BOUND),
            VMEM,
            VMEM,
        ],
        out_specs=(VMEM, VMEM, VMEM),
        scratch_shapes=[pltpu.VMEM((size, width), jnp.bfloat16), pltpu.VMEM((ROWS, width), jnp.float32)],
        compiler_params=pltpu.CompilerParams(vmem_limit_bytes=24 * 1024 * 1024),
        cost_estimate=pl.CostEstimate(
            flops=2 * size * size * width, bytes_accessed=2 * size * size + 20 * HEAD * width, transcendentals=0
        ),
        name="follow",
    )(matrix, costs, costs, low, high, head, v_full, rest)


def unwritten(*shape):
    return pl.pallas_call(lambda out: None, out_shape=f32(*shape), out_specs=HBM, name="unwritten")()


def transfers(couple, ends, colour, *rest):
    areas = lax.axis_size("area")
    windows = lax.axis_size("win")
    onward = [(i, i + 1) for i in range(windows - 1)]

    def swap(bits):
        def branch(c, e, *rest):
            if bits:
                other = lax.ppermute(c, "area", [(i, i ^ bits) for i in range(areas)])
            else:
                other = unwritten(*c.shape)
            return (other, lax.ppermute(e, "win", onward), *follow(*rest))

        return branch

    return lax.switch(colour, [swap(bits) for bits in range(areas)], couple, ends, *rest)


def finish_kernel(code, low, high, head, tail, other, before, z_out, u_out):
    linked = (code[0] & (2**BITS - 1)) > 0
    block = pl.program_id(0)

    def put(t, join):
        z = join(clip(t, low[...], high[...]))
        z_out[...] = z
        u_out[...] = t - z

    @pl.when(block < COUPLE // ROWS)
    def _():
        put(head[...], lambda y: jnp.where(linked, y + 0.5 * (other[...] - y), y))

    @pl.when((block >= COUPLE // ROWS) & (block < HEAD // ROWS))
    def _():
        put(head[...], lambda y: y)

    @pl.when(block == HEAD // ROWS)
    def _():
        put(tail[...], lambda y: 0.5 * (y + before[...]))

    @pl.when(block > HEAD // ROWS)
    def _():
        put(tail[...], lambda y: y)


def finish(code, low, high, head, tail, other, before):
    size, width = low.shape[0], head.shape[1]
    block = lambda index: pl.BlockSpec((ROWS, width), lambda i: (index(i), 0))
    bound = pl.BlockSpec((ROWS, LANES), lambda i: (i, 0))
    return pl.pallas_call(
        finish_kernel,
        out_shape=(f32(size, width), f32(size, width)),
        grid=(size // ROWS,),
        in_specs=[
            SMEM,
            bound,
            bound,
            block(lambda i: jnp.minimum(i, HEAD // ROWS - 1)),
            block(lambda i: jnp.maximum(i - HEAD // ROWS, 0)),
            block(lambda i: jnp.minimum(i, COUPLE // ROWS - 1)),
            block(lambda i: 0),
        ],
        out_specs=(block(lambda i: i), block(lambda i: i)),
        name="finish",
    )(code, low, high, head, tail, other, before)


def local(kkt, offsets, lower, upper, partners, adjacency):
    matrix = kkt[0, 0]
    costs = offsets[0, 0]
    area = lax.axis_index("area")[None].astype(jnp.int32)
    code, low, high, v_own, partial, head, tail, other, before = prepare(
        area, partners, adjacency, lower[0], upper[0], matrix, costs
    )

    def iterate(carry):
        code, head, tail, v_own, partial, other, before = carry
        head, couple, ends, v_full, rest = lead(
            code[None], matrix, costs, low, high, head, tail, v_own, partial, other, before
        )
        code = code >> BITS
        other, before, tail, v_own, partial = transfers(
            couple, ends, code & (2**BITS - 1), matrix, costs, low, high, head, v_full, rest
        )
        return code, head, tail, v_own, partial, other, before

    more = lambda carry: carry[0] >= 1 << (BITS + 1)
    carry = (code[0], head, tail, v_own, partial, other, before)
    code, head, tail, _, _, other, before = lax.while_loop(more, iterate, carry)
    z_now, u_now = finish(code[None], low, high, head, tail, other, before)
    return (z_now[None, None], u_now[None, None])


def solution(mesh):
    in_specs = (
        P("area", "win", None, None),
        P("area", "win", None, None),
        P("area", "win", None),
        P("area", "win", None),
        P(),
        P(),
    )
    out_specs = (P("area", "win", None, None), P("area", "win", None, None))
    return jax.shard_map(local, mesh=mesh, in_specs=in_specs, out_specs=out_specs, check_vma=False)
```

```python
import jax
import jax.numpy as jnp
from jax import lax
from jax.experimental import pallas as pl
from jax.experimental.pallas import tpu as pltpu
from jax.sharding import PartitionSpec as P

COUPLE = 512
BOUND = 256
HEAD = COUPLE + BOUND
ITERS = 4
ROWS = 256
LANES = 128
BITS = 5
CHUNK = 64

HBM = pl.BlockSpec(memory_space=pltpu.HBM)
VMEM = pl.BlockSpec(memory_space=pltpu.VMEM)
SMEM = pl.BlockSpec(memory_space=pltpu.SMEM)


def f32(*shape):
    return jax.ShapeDtypeStruct(shape, jnp.float32)


def bf16(*shape):
    return jax.ShapeDtypeStruct(shape, jnp.bfloat16)


WORD = jax.ShapeDtypeStruct((1,), jnp.int32)
WORDS = jax.ShapeDtypeStruct((8, LANES), jnp.int32)


def clip(total, low, high):
    width = total.shape[1] // LANES
    low, high = (jnp.concatenate([b] * width, axis=1) for b in (low, high))
    return jnp.minimum(jnp.maximum(total, low), high)


def product(left, right):
    return jnp.dot(left, right, preferred_element_type=jnp.float32)


def prepare_kernel(
    area, partners_hbm, adjacency_hbm, lower_hbm, upper_hbm, matrix_hbm, costs_hbm,
    code, words, low, high, v_own_out, partial_out, head_out, tail_out, before_out, other_out,
    zero, partners, adjacency, lower, upper, matrix, costs, v_own, partial, sems,
):
    others = costs_hbm.shape[0] - HEAD - BOUND
    end, other = pl.ds(COUPLE, BOUND), pl.ds(HEAD + BOUND, others)
    own_end, own_other = pl.ds(0, BOUND), pl.ds(BOUND, others)
    small = [
        move(lower_hbm, lower, sems.at[0]),
        move(upper_hbm, upper, sems.at[1]),
        move(partners_hbm, partners, sems.at[2]),
        move(adjacency_hbm, adjacency, sems.at[3]),
    ]
    values = [
        move(costs_hbm.at[end, :], costs.at[own_end, :], sems.at[4]),
        move(costs_hbm.at[other, :], costs.at[own_other, :], sems.at[5]),
    ]
    weights = [
        move(matrix_hbm.at[pl.ds(0, HEAD), end], matrix.at[:, own_end], sems.at[6]),
        move(matrix_hbm.at[pl.ds(0, HEAD), other], matrix.at[:, own_other], sems.at[7]),
    ]
    for copy in small + values + weights:
        copy.start()
    zero[...] = jnp.zeros_like(zero)
    out = [
        move(zero, head_out, sems.at[8]),
        move(zero, tail_out, sems.at[9]),
        move(zero.at[pl.ds(0, BOUND), :], before_out, sems.at[10]),
    ]
    for copy in out:
        copy.start()
    for copy in small:
        copy.wait()
    packed = 1 << (BITS * (ITERS + 1))
    for k in range(ITERS):
        linked = adjacency[area[0], partners[k, area[0]]] == 1
        packed = packed + (jnp.where(linked, partners[k, 0], 0) << (BITS * (k + 1)))
    code[0] = packed
    words[...] = jnp.full(words.shape, packed, jnp.int32)
    for source, target in ((lower, low), (upper, high)):
        for start in range(0, source.shape[1], LANES):
            line = source[0:1, start : start + LANES]
            target[start : start + LANES, :] = jnp.broadcast_to(line, (LANES, LANES)).T
    for copy in values:
        copy.wait()
    v_own[...] = costs[...].astype(jnp.bfloat16)
    out.append(move(v_own, v_own_out, sems.at[11]))
    out[-1].start()
    for copy in weights:
        copy.wait()
    for at in range(0, HEAD, ROWS):
        rows = pl.ds(at, ROWS)
        partial[rows, :] = product(matrix[rows, :], v_own[...])
        out.append(move(partial.at[rows, :], partial_out.at[rows, :], sems.at[12 + at // ROWS]))
        out[-1].start()
    for copy in out:
        copy.wait()


def prepare(area, partners, adjacency, lower, upper, matrix, costs):
    size, width = costs.shape
    rest = size - HEAD
    return pl.pallas_call(
        prepare_kernel,
        out_shape=(WORD, WORDS, f32(size, LANES), f32(size, LANES), bf16(rest, width), f32(HEAD, width),
                   f32(HEAD, width), f32(rest, width), f32(BOUND, width), f32(COUPLE, width)),
        in_specs=[SMEM] + [HBM] * 6,
        out_specs=(SMEM, VMEM, VMEM, VMEM) + (HBM,) * 6,
        scratch_shapes=[
            pltpu.VMEM((HEAD, width), jnp.float32),
            pltpu.SMEM(partners.shape, jnp.int32),
            pltpu.SMEM(adjacency.shape, jnp.int32),
            pltpu.VMEM(lower.shape, jnp.float32),
            pltpu.VMEM(upper.shape, jnp.float32),
            pltpu.VMEM((HEAD, rest), matrix.dtype),
            pltpu.VMEM((rest, width), jnp.float32),
            pltpu.VMEM((rest, width), jnp.bfloat16),
            pltpu.VMEM((HEAD, width), jnp.float32),
            pltpu.SemaphoreType.DMA((12 + HEAD // ROWS,)),
        ],
        name="prepare",
    )(area, partners, adjacency, lower, upper, matrix, costs)


def move(source, target, sem):
    return pltpu.make_async_copy(source, target, sem)


def lead_kernel(
    words_hbm, matrix_hbm, costs_hbm, low, high, head_hbm, tail_hbm, partial_hbm, other_hbm, before_hbm,
    head_out, couple_out, ends_out, v_out, u_out, words_out, code_out, colour_out,
    head, start, matrix, matrix_start, costs, total, other, before, v_ref, sent, words, coded, colour, sems,
):
    couples, starts = pl.ds(0, COUPLE), pl.ds(HEAD, BOUND)
    read = move(words_hbm, words, sems.at[11])
    first = [
        move(head_hbm.at[couples, :], head, sems.at[0]),
        move(other_hbm, other, sems.at[1]),
        move(costs_hbm.at[couples, :], costs.at[couples, :], sems.at[2]),
    ]
    second = [
        move(tail_hbm.at[pl.ds(0, BOUND), :], start, sems.at[3]),
        move(before_hbm, before, sems.at[4]),
        move(costs_hbm.at[starts, :], costs.at[pl.ds(COUPLE, BOUND), :], sems.at[5]),
    ]
    third = [
        move(matrix_hbm.at[pl.ds(0, HEAD), couples], matrix, sems.at[6]),
        move(matrix_hbm.at[pl.ds(0, HEAD), starts], matrix_start, sems.at[7]),
        move(partial_hbm, total, sems.at[8]),
    ]
    for copy in [read] + first + second + third:
        copy.start()
    read.wait()
    code = jnp.max(words[...])
    linked = (code & (2**BITS - 1)) > 0
    coded[0] = code >> BITS
    colour[0] = (code >> BITS) & (2**BITS - 1)
    words[...] = words[...] >> BITS
    out = [
        move(words, words_out, sems.at[12]),
        move(coded, code_out, sems.at[13]),
        move(colour, colour_out, sems.at[14]),
    ]
    for copy in out:
        copy.start()
    for copy in first:
        copy.wait()
    for at in range(0, COUPLE, ROWS):
        rows = slice(at, at + ROWS)
        t = head[rows, :]
        y = clip(t, low[rows, :], high[rows, :])
        z = jnp.where(linked, y + 0.5 * (other[rows, :] - y), y)
        u = t - z
        v_ref[rows, :] = (costs[rows, :] + z - u).astype(jnp.bfloat16)
        head[rows, :] = u
    for copy in second:
        copy.wait()
    rows = slice(HEAD, HEAD + BOUND)
    t = start[...]
    z = 0.5 * (clip(t, low[rows, :], high[rows, :]) + before[...])
    u = t - z
    v_ref[COUPLE:, :] = (costs[COUPLE:, :] + z - u).astype(jnp.bfloat16)
    start[...] = u
    now = [move(v_ref, v_out, sems.at[9]), move(start, u_out, sems.at[10])]
    for copy in now:
        copy.start()
    out += now
    for copy in third:
        copy.wait()
    for at in range(0, HEAD, ROWS):
        rows, block = slice(at, at + ROWS), pl.ds(at, ROWS)
        x = product(matrix[rows, :], v_ref[:COUPLE, :]) + product(matrix_start[rows, :], v_ref[COUPLE:, :])
        t = total[rows, :] + x
        if at < COUPLE:
            t = head[rows, :] + t
        total[rows, :] = t
        sent[rows, :] = clip(t, low[rows, :], high[rows, :])
        target = couple_out.at[block, :] if at < COUPLE else ends_out
        now = [
            move(sent.at[block, :], target, sems.at[15 + 2 * at // ROWS]),
            move(total.at[block, :], head_out.at[block, :], sems.at[16 + 2 * at // ROWS]),
        ]
        for copy in now:
            copy.start()
        out += now
    for copy in out:
        copy.wait()


def lead(words, matrix, costs, low, high, head, tail, partial, other, before):
    width = costs.shape[1]
    return pl.pallas_call(
        lead_kernel,
        out_shape=(f32(HEAD, width), f32(COUPLE, width), f32(BOUND, width), bf16(HEAD, width), f32(BOUND, width),
                   WORDS, WORD, WORD),
        in_specs=[HBM, HBM, HBM, VMEM, VMEM] + [HBM] * 5,
        out_specs=(HBM,) * 8,
        input_output_aliases={5: 0, 0: 5},
        scratch_shapes=[
            pltpu.VMEM((COUPLE, width), jnp.float32),
            pltpu.VMEM((BOUND, width), jnp.float32),
            pltpu.VMEM((HEAD, COUPLE), matrix.dtype),
            pltpu.VMEM((HEAD, BOUND), matrix.dtype),
            pltpu.VMEM((HEAD, width), jnp.float32),
            pltpu.VMEM((HEAD, width), jnp.float32),
            pltpu.VMEM((COUPLE, width), jnp.float32),
            pltpu.VMEM((BOUND, width), jnp.float32),
            pltpu.VMEM((HEAD, width), jnp.bfloat16),
            pltpu.VMEM((HEAD, width), jnp.float32),
            pltpu.VMEM(WORDS.shape, jnp.int32),
            pltpu.SMEM((1,), jnp.int32),
            pltpu.SMEM((1,), jnp.int32),
            pltpu.SemaphoreType.DMA((15 + 2 * HEAD // ROWS,)),
        ],
        compiler_params=pltpu.CompilerParams(vmem_limit_bytes=24 * 1024 * 1024),
        cost_estimate=pl.CostEstimate(
            flops=2 * HEAD * HEAD * width, bytes_accessed=2 * HEAD * HEAD + 30 * HEAD * width, transcendentals=0
        ),
        name="lead",
    )(words, matrix, costs, low, high, head, tail, partial, other, before)


def follow_kernel(
    matrix_hbm, costs_hbm, low, high, head_hbm, tail_hbm, v_own_hbm, v_new_hbm, u_start_hbm,
    tail_out, v_own_out, partial_out, matrix, v_ref, total, costs, sems,
):
    size = total.shape[0]
    others = size - HEAD - BOUND
    couple, end, start, other = (
        pl.ds(0, COUPLE), pl.ds(COUPLE, BOUND), pl.ds(HEAD, BOUND), pl.ds(HEAD + BOUND, others)
    )
    own_end, own_other = pl.ds(0, BOUND), pl.ds(BOUND, others)
    heads, parts = HEAD // ROWS, size // COUPLE

    def block(r):
        return pl.ds(pl.multiple_of(r * ROWS, ROWS), ROWS)

    def fetch(r):
        return move(matrix_hbm.at[block(r), :], matrix.at[block(r), :], sems.at[0, r])

    vectors = [
        move(v_new_hbm.at[couple, :], v_ref.at[couple, :], sems.at[1, 0]),
        move(v_new_hbm.at[pl.ds(COUPLE, BOUND), :], v_ref.at[start, :], sems.at[1, 1]),
        move(v_own_hbm.at[own_end, :], v_ref.at[end, :], sems.at[1, 2]),
        move(v_own_hbm.at[own_other, :], v_ref.at[other, :], sems.at[1, 3]),
        move(u_start_hbm, total.at[start, :], sems.at[1, 4]),
        move(tail_hbm.at[own_other, :], total.at[other, :], sems.at[1, 5]),
    ]
    later = [
        move(head_hbm.at[end, :], total.at[end, :], sems.at[2, 0]),
        move(costs_hbm.at[end, :], costs.at[own_end, :], sems.at[2, 1]),
        move(costs_hbm.at[other, :], costs.at[own_other, :], sems.at[2, 2]),
    ]
    own_back = [
        move(v_ref.at[end, :], v_own_out.at[own_end, :], sems.at[2, 3]),
        move(v_ref.at[other, :], v_own_out.at[own_other, :], sems.at[2, 4]),
    ]

    def tail_back(r):
        return move(total.at[block(r), :], tail_out.at[block(r - heads), :], sems.at[3, r])

    def partial_back(r):
        return move(total.at[block(r), :], partial_out.at[block(r), :], sems.at[3, r])

    for copy in vectors:
        copy.start()

    @pl.loop(heads, 2 * heads)
    def _(r):
        fetch(r).start()

    for copy in later:
        copy.start()

    @pl.loop(0, heads)
    def _(r):
        fetch(r).start()

    def bounded(t, at):
        return clip(t, low[at, :], high[at, :])

    for copy in vectors:
        copy.wait()

    @pl.loop(0, others // CHUNK)
    def _(c):
        at = pl.ds(pl.multiple_of(HEAD + BOUND + c * CHUNK, CHUNK), CHUNK)
        t = total[at, :]
        total[at, :] = t - bounded(t, at)

    first = heads * parts

    @pl.loop(0, first + heads * (parts - 1))
    def _(w):
        early = w < first
        r = jnp.where(early, heads + w // parts, (w - first) // (parts - 1))
        j = jnp.where(early, w % parts, 1 + (w - first) % (parts - 1))

        @pl.when(w == first)
        def _():
            for copy in later:
                copy.wait()

            @pl.loop(0, (BOUND + others) // CHUNK)
            def _(c):
                is_end = c < BOUND // CHUNK
                own = pl.ds(pl.multiple_of(c * CHUNK, CHUNK), CHUNK)
                at = pl.ds(pl.multiple_of(c * CHUNK + jnp.where(is_end, COUPLE, HEAD), CHUNK), CHUNK)
                t = total[at, :]
                y = bounded(t, at)
                u = t - y
                v_ref[at, :] = (costs[own, :] + y - u).astype(jnp.bfloat16)

                @pl.when(is_end)
                def _():
                    total[at, :] = u

            for copy in own_back:
                copy.start()
            v_ref[start, :] = jnp.zeros((BOUND, v_ref.shape[1]), jnp.bfloat16)

            @pl.loop(0, COUPLE // CHUNK)
            def _(c):
                at = pl.ds(pl.multiple_of(c * CHUNK, CHUNK), CHUNK)
                total[at, :] = jnp.zeros((CHUNK, total.shape[1]), jnp.float32)

        @pl.when(j == jnp.where(early, 0, 1))
        def _():
            fetch(r).wait()

        cut = pl.ds(pl.multiple_of(j * COUPLE, COUPLE), COUPLE)
        total[block(r), :] += product(matrix[block(r), cut], v_ref[cut, :])

        @pl.when((j == parts - 1) & early)
        def _():
            tail_back(r).start()

        @pl.when((j == parts - 1) & jnp.logical_not(early))
        def _():
            partial_back(r).start()

    @pl.loop(heads, 2 * heads)
    def _(r):
        tail_back(r).wait()

    for copy in own_back:
        copy.wait()

    @pl.loop(0, heads)
    def _(r):
        partial_back(r).wait()


def follow(matrix, costs, low, high, head, tail, v_own, v_new, u_start):
    size, width = costs.shape
    return pl.pallas_call(
        follow_kernel,
        out_shape=(f32(*tail.shape), bf16(*v_own.shape), f32(HEAD, width)),
        in_specs=[HBM, HBM, VMEM, VMEM] + [HBM] * 5,
        out_specs=(HBM,) * 3,
        input_output_aliases={5: 0, 6: 1},
        scratch_shapes=[
            pltpu.VMEM(matrix.shape, matrix.dtype),
            pltpu.VMEM((size, width), jnp.bfloat16),
            pltpu.VMEM((size, width), jnp.float32),
            pltpu.VMEM(tail.shape, jnp.float32),
            pltpu.SemaphoreType.DMA((4, size // ROWS)),
        ],
        compiler_params=pltpu.CompilerParams(vmem_limit_bytes=24 * 1024 * 1024),
        cost_estimate=pl.CostEstimate(
            flops=2 * size * size * width, bytes_accessed=2 * size * size + 20 * HEAD * width, transcendentals=0
        ),
        name="follow",
    )(matrix, costs, low, high, head, tail, v_own, v_new, u_start)


def unwritten(*shape):
    return pl.pallas_call(lambda out: None, out_shape=f32(*shape), out_specs=HBM, name="unwritten")()


def transfers(couple, ends, colour, *rest):
    areas = lax.axis_size("area")
    windows = lax.axis_size("win")
    onward = [(i, i + 1) for i in range(windows - 1)]

    def swap(bits):
        def branch(c, e, *rest):
            if bits:
                other = lax.ppermute(c, "area", [(i, i ^ bits) for i in range(areas)])
            else:
                other = unwritten(*c.shape)
            return (other, lax.ppermute(e, "win", onward), *follow(*rest))

        return branch

    return lax.switch(colour, [swap(bits) for bits in range(areas)], couple, ends, *rest)


def finish_kernel(
    code, low, high, head_hbm, tail_hbm, other_hbm, before_hbm, z_out, u_out, total, joined, sems
):
    blocks, heads = total.shape[0] // ROWS, HEAD // ROWS
    at = lambda i: pl.ds(i * ROWS, ROWS)
    totals, joins = [], {}
    for i in range(blocks):
        source = head_hbm.at[at(i), :] if i < heads else tail_hbm.at[at(i - heads), :]
        totals.append(move(source, total.at[at(i), :], sems.at[0, i]))
        totals[i].start()
        if i < COUPLE // ROWS or i == heads:
            source = before_hbm if i == heads else other_hbm.at[at(i), :]
            joins[i] = move(source, joined.at[at(i), :], sems.at[1, i])
            joins[i].start()
    linked = (code[0] & (2**BITS - 1)) > 0
    out = []
    for i in range(blocks):
        rows = slice(i * ROWS, (i + 1) * ROWS)
        totals[i].wait()
        t = total[rows, :]
        z = clip(t, low[rows, :], high[rows, :])
        if i in joins:
            joins[i].wait()
            other = joined[rows, :]
            z = 0.5 * (z + other) if i == heads else jnp.where(linked, z + 0.5 * (other - z), z)
        joined[rows, :] = z
        total[rows, :] = t - z
        now = [
            move(joined.at[at(i), :], z_out.at[at(i), :], sems.at[2, i]),
            move(total.at[at(i), :], u_out.at[at(i), :], sems.at[3, i]),
        ]
        for copy in now:
            copy.start()
        out += now
    for copy in out:
        copy.wait()


def finish(code, low, high, head, tail, other, before):
    size, width = low.shape[0], head.shape[1]
    return pl.pallas_call(
        finish_kernel,
        out_shape=(f32(size, width), f32(size, width)),
        in_specs=[SMEM, VMEM, VMEM] + [HBM] * 4,
        out_specs=(HBM, HBM),
        scratch_shapes=[
            pltpu.VMEM((size, width), jnp.float32),
            pltpu.VMEM((size, width), jnp.float32),
            pltpu.SemaphoreType.DMA((4, size // ROWS)),
        ],
        name="finish",
    )(code, low, high, head, tail, other, before)


def local(kkt, offsets, lower, upper, partners, adjacency):
    matrix = kkt[0, 0]
    costs = offsets[0, 0]
    area = lax.axis_index("area")[None].astype(jnp.int32)
    code, words, low, high, v_own, partial, head, tail, before, other = prepare(
        area, partners, adjacency, lower[0], upper[0], matrix, costs
    )

    def iterate(carry):
        _, words, head, tail, v_own, partial, other, before = carry
        head, couple, ends, v_new, u_start, words, code, colour = lead(
            words, matrix, costs, low, high, head, tail, partial, other, before
        )
        other, before, tail, v_own, partial = transfers(
            couple, ends, colour[0], matrix, costs, low, high, head, tail, v_own, v_new, u_start
        )
        return code, words, head, tail, v_own, partial, other, before

    more = lambda carry: carry[0][0] >= 1 << (BITS + 1)
    carry = (code, words, head, tail, v_own, partial, other, before)
    code, _, head, tail, _, _, other, before = lax.while_loop(more, iterate, carry)
    z_now, u_now = finish(code, low, high, head, tail, other, before)
    return (z_now[None, None], u_now[None, None])


def solution(mesh):
    in_specs = (
        P("area", "win", None, None),
        P("area", "win", None, None),
        P("area", "win", None),
        P("area", "win", None),
        P(),
        P(),
    )
    out_specs = (P("area", "win", None, None), P("area", "win", None, None))
    return jax.shard_map(local, mesh=mesh, in_specs=in_specs, out_specs=out_specs, check_vma=False)
```

```python
import jax
import jax.numpy as jnp
from jax import lax
from jax.experimental import pallas as pl
from jax.experimental.pallas import tpu as pltpu
from jax.sharding import PartitionSpec as P

COUPLE = 512
BOUND = 256
HEAD = COUPLE + BOUND
ITERS = 4
ROWS = 256
LANES = 128
BITS = 5
CHUNK = 64

HBM = pl.BlockSpec(memory_space=pltpu.HBM)
VMEM = pl.BlockSpec(memory_space=pltpu.VMEM)
SMEM = pl.BlockSpec(memory_space=pltpu.SMEM)


def f32(*shape):
    return jax.ShapeDtypeStruct(shape, jnp.float32)


def bf16(*shape):
    return jax.ShapeDtypeStruct(shape, jnp.bfloat16)


WORD = jax.ShapeDtypeStruct((1,), jnp.int32)
WORDS = jax.ShapeDtypeStruct((8, LANES), jnp.int32)


def clip(total, low, high):
    width = total.shape[1] // LANES
    low, high = (jnp.concatenate([b] * width, axis=1) for b in (low, high))
    return jnp.minimum(jnp.maximum(total, low), high)


def product(left, right):
    return jnp.dot(left, right, preferred_element_type=jnp.float32)


def prepare_kernel(
    area, partners_hbm, adjacency_hbm, lower_hbm, upper_hbm, matrix_hbm, costs_hbm,
    code, words, low, high, v_own_out, partial_out, head_out, tail_out, before_out, other_out,
    zero, partners, adjacency, lower, upper, matrix, costs, v_own, partial, sems,
):
    others = costs_hbm.shape[0] - HEAD - BOUND
    end, other = pl.ds(COUPLE, BOUND), pl.ds(HEAD + BOUND, others)
    own_end, own_other = pl.ds(0, BOUND), pl.ds(BOUND, others)
    small = [
        move(lower_hbm, lower, sems.at[0]),
        move(upper_hbm, upper, sems.at[1]),
        move(partners_hbm, partners, sems.at[2]),
        move(adjacency_hbm, adjacency, sems.at[3]),
    ]
    values = [
        move(costs_hbm.at[end, :], costs.at[own_end, :], sems.at[4]),
        move(costs_hbm.at[other, :], costs.at[own_other, :], sems.at[5]),
    ]
    weights = [
        move(matrix_hbm.at[pl.ds(0, HEAD), end], matrix.at[:, own_end], sems.at[6]),
        move(matrix_hbm.at[pl.ds(0, HEAD), other], matrix.at[:, own_other], sems.at[7]),
    ]
    for copy in small + values + weights:
        copy.start()
    zero[...] = jnp.zeros_like(zero)
    out = [
        move(zero, head_out, sems.at[8]),
        move(zero, tail_out, sems.at[9]),
        move(zero.at[pl.ds(0, BOUND), :], before_out, sems.at[10]),
    ]
    for copy in out:
        copy.start()
    for copy in values:
        copy.wait()
    v_own[...] = costs[...].astype(jnp.bfloat16)
    out.append(move(v_own, v_own_out, sems.at[11]))
    out[-1].start()
    for copy in weights:
        copy.wait()
    for at in range(0, HEAD, ROWS):
        rows = pl.ds(at, ROWS)
        partial[rows, :] = product(matrix[rows, :], v_own[...])
        out.append(move(partial.at[rows, :], partial_out.at[rows, :], sems.at[12 + at // ROWS]))
        out[-1].start()
    for copy in small:
        copy.wait()
    packed = 1 << (BITS * (ITERS + 1))
    for k in range(ITERS):
        linked = adjacency[area[0], partners[k, area[0]]] == 1
        packed = packed + (jnp.where(linked, partners[k, 0], 0) << (BITS * (k + 1)))
    code[0] = packed
    words[...] = jnp.full(words.shape, packed, jnp.int32)
    for source, target in ((lower, low), (upper, high)):
        for start in range(0, source.shape[1], LANES):
            line = source[0:1, start : start + LANES]
            target[start : start + LANES, :] = jnp.broadcast_to(line, (LANES, LANES)).T
    for copy in out:
        copy.wait()


def prepare(area, partners, adjacency, lower, upper, matrix, costs):
    size, width = costs.shape
    rest = size - HEAD
    return pl.pallas_call(
        prepare_kernel,
        out_shape=(WORD, WORDS, f32(size, LANES), f32(size, LANES), bf16(rest, width), f32(HEAD, width),
                   f32(HEAD, width), f32(rest, width), f32(BOUND, width), f32(COUPLE, width)),
        in_specs=[SMEM] + [HBM] * 6,
        out_specs=(SMEM, VMEM, VMEM, VMEM) + (HBM,) * 6,
        scratch_shapes=[
            pltpu.VMEM((HEAD, width), jnp.float32),
            pltpu.SMEM(partners.shape, jnp.int32),
            pltpu.SMEM(adjacency.shape, jnp.int32),
            pltpu.VMEM(lower.shape, jnp.float32),
            pltpu.VMEM(upper.shape, jnp.float32),
            pltpu.VMEM((HEAD, rest), matrix.dtype),
            pltpu.VMEM((rest, width), jnp.float32),
            pltpu.VMEM((rest, width), jnp.bfloat16),
            pltpu.VMEM((HEAD, width), jnp.float32),
            pltpu.SemaphoreType.DMA((12 + HEAD // ROWS,)),
        ],
        name="prepare",
    )(area, partners, adjacency, lower, upper, matrix, costs)


def move(source, target, sem):
    return pltpu.make_async_copy(source, target, sem)


def lead_kernel(
    words, matrix_hbm, costs, low, high, head_hbm, tail_hbm, partial_hbm, other_hbm, before_hbm,
    head_out, couple_out, ends_out, v_ref, u_out, words_out, code_out, colour_out,
    head, start, matrix, matrix_start, total, other, before, sent, coded, colour, sems,
):
    couples, starts = pl.ds(0, COUPLE), pl.ds(HEAD, BOUND)
    first = [
        move(head_hbm.at[couples, :], head, sems.at[0]),
        move(other_hbm, other, sems.at[1]),
    ]
    second = [
        move(tail_hbm.at[pl.ds(0, BOUND), :], start, sems.at[3]),
        move(before_hbm, before, sems.at[4]),
    ]
    third = [
        move(matrix_hbm.at[pl.ds(0, HEAD), couples], matrix, sems.at[6]),
        move(matrix_hbm.at[pl.ds(0, HEAD), starts], matrix_start, sems.at[7]),
        move(partial_hbm, total, sems.at[8]),
    ]
    for copy in first + second + third:
        copy.start()
    code = jnp.max(words[...])
    linked = (code & (2**BITS - 1)) > 0
    coded[0] = code >> BITS
    colour[0] = (code >> BITS) & (2**BITS - 1)
    words_out[...] = words[...] >> BITS
    out = [
        move(coded, code_out, sems.at[13]),
        move(colour, colour_out, sems.at[14]),
    ]
    for copy in out:
        copy.start()
    for copy in first:
        copy.wait()
    for at in range(0, COUPLE, ROWS):
        rows = slice(at, at + ROWS)
        t = head[rows, :]
        y = clip(t, low[rows, :], high[rows, :])
        z = jnp.where(linked, y + 0.5 * (other[rows, :] - y), y)
        u = t - z
        v_ref[rows, :] = (costs[rows, :] + z - u).astype(jnp.bfloat16)
        head[rows, :] = u
    for copy in second:
        copy.wait()
    rows = slice(HEAD, HEAD + BOUND)
    t = start[...]
    z = 0.5 * (clip(t, low[rows, :], high[rows, :]) + before[...])
    u = t - z
    v_ref[COUPLE:, :] = (costs[rows, :] + z - u).astype(jnp.bfloat16)
    start[...] = u
    out.append(move(start, u_out, sems.at[10]))
    out[-1].start()
    for copy in third:
        copy.wait()
    for at in range(0, HEAD, ROWS):
        rows, block = slice(at, at + ROWS), pl.ds(at, ROWS)
        x = product(matrix[rows, :], v_ref[:COUPLE, :]) + product(matrix_start[rows, :], v_ref[COUPLE:, :])
        t = total[rows, :] + x
        if at < COUPLE:
            t = head[rows, :] + t
        total[rows, :] = t
        sent[rows, :] = clip(t, low[rows, :], high[rows, :])
        target = couple_out.at[block, :] if at < COUPLE else ends_out
        now = [
            move(sent.at[block, :], target, sems.at[15 + 2 * at // ROWS]),
            move(total.at[block, :], head_out.at[block, :], sems.at[16 + 2 * at // ROWS]),
        ]
        for copy in now:
            copy.start()
        out += now
    for copy in out:
        copy.wait()


def lead(words, matrix, costs, low, high, head, tail, partial, other, before):
    width = costs.shape[1]
    return pl.pallas_call(
        lead_kernel,
        out_shape=(f32(HEAD, width), f32(COUPLE, width), f32(BOUND, width), bf16(HEAD, width), f32(BOUND, width),
                   WORDS, WORD, WORD),
        in_specs=[VMEM, HBM, VMEM, VMEM, VMEM] + [HBM] * 5,
        out_specs=(HBM, HBM, HBM, VMEM, HBM, VMEM, HBM, HBM),
        input_output_aliases={5: 0, 0: 5},
        scratch_shapes=[
            pltpu.VMEM((COUPLE, width), jnp.float32),
            pltpu.VMEM((BOUND, width), jnp.float32),
            pltpu.VMEM((HEAD, COUPLE), matrix.dtype),
            pltpu.VMEM((HEAD, BOUND), matrix.dtype),
            pltpu.VMEM((HEAD, width), jnp.float32),
            pltpu.VMEM((COUPLE, width), jnp.float32),
            pltpu.VMEM((BOUND, width), jnp.float32),
            pltpu.VMEM((HEAD, width), jnp.float32),
            pltpu.SMEM((1,), jnp.int32),
            pltpu.SMEM((1,), jnp.int32),
            pltpu.SemaphoreType.DMA((15 + 2 * HEAD // ROWS,)),
        ],
        compiler_params=pltpu.CompilerParams(vmem_limit_bytes=24 * 1024 * 1024),
        cost_estimate=pl.CostEstimate(
            flops=2 * HEAD * HEAD * width, bytes_accessed=2 * HEAD * HEAD + 30 * HEAD * width, transcendentals=0
        ),
        name="lead",
    )(words, matrix, costs, low, high, head, tail, partial, other, before)


def follow_kernel(
    matrix_hbm, costs, low, high, head_hbm, tail_hbm, v_own_hbm, v_new, u_start_hbm,
    tail_out, v_own_out, partial_out, matrix, v_ref, total, sems,
):
    size = total.shape[0]
    others = size - HEAD - BOUND
    couple, end, start, other = (
        pl.ds(0, COUPLE), pl.ds(COUPLE, BOUND), pl.ds(HEAD, BOUND), pl.ds(HEAD + BOUND, others)
    )
    own_end, own_other = pl.ds(0, BOUND), pl.ds(BOUND, others)
    heads, parts = HEAD // ROWS, size // COUPLE

    def block(r):
        return pl.ds(pl.multiple_of(r * ROWS, ROWS), ROWS)

    def fetch(r):
        return move(matrix_hbm.at[block(r), :], matrix.at[block(r), :], sems.at[0, r])

    vectors = [
        move(v_own_hbm.at[own_end, :], v_ref.at[end, :], sems.at[1, 2]),
        move(v_own_hbm.at[own_other, :], v_ref.at[other, :], sems.at[1, 3]),
        move(u_start_hbm, total.at[start, :], sems.at[1, 4]),
        move(tail_hbm.at[own_other, :], total.at[other, :], sems.at[1, 5]),
    ]
    later = [move(head_hbm.at[end, :], total.at[end, :], sems.at[2, 0])]
    own_back = [
        move(v_ref.at[end, :], v_own_out.at[own_end, :], sems.at[2, 3]),
        move(v_ref.at[other, :], v_own_out.at[own_other, :], sems.at[2, 4]),
    ]

    def tail_back(r):
        return move(total.at[block(r), :], tail_out.at[block(r - heads), :], sems.at[3, r])

    def partial_back(r):
        return move(total.at[block(r), :], partial_out.at[block(r), :], sems.at[3, r])

    for copy in vectors:
        copy.start()

    @pl.loop(heads, 2 * heads)
    def _(r):
        fetch(r).start()

    for copy in later:
        copy.start()

    @pl.loop(0, heads)
    def _(r):
        fetch(r).start()

    def bounded(t, at):
        return clip(t, low[at, :], high[at, :])

    @pl.loop(0, HEAD // CHUNK)
    def _(c):
        at = pl.ds(pl.multiple_of(c * CHUNK, CHUNK), CHUNK)
        to = pl.ds(pl.multiple_of(c * CHUNK + jnp.where(c < COUPLE // CHUNK, 0, BOUND), CHUNK), CHUNK)
        v_ref[to, :] = v_new[at, :]

    for copy in vectors:
        copy.wait()

    @pl.loop(0, others // CHUNK)
    def _(c):
        at = pl.ds(pl.multiple_of(HEAD + BOUND + c * CHUNK, CHUNK), CHUNK)
        t = total[at, :]
        total[at, :] = t - bounded(t, at)

    first = heads * parts

    @pl.loop(0, first + heads * (parts - 1))
    def _(w):
        early = w < first
        r = jnp.where(early, heads + w // parts, (w - first) // (parts - 1))
        j = jnp.where(early, w % parts, 1 + (w - first) % (parts - 1))

        @pl.when(w == first)
        def _():
            for copy in later:
                copy.wait()

            @pl.loop(0, (BOUND + others) // CHUNK)
            def _(c):
                is_end = c < BOUND // CHUNK
                at = pl.ds(pl.multiple_of(c * CHUNK + jnp.where(is_end, COUPLE, HEAD), CHUNK), CHUNK)
                t = total[at, :]
                y = bounded(t, at)
                u = t - y
                v_ref[at, :] = (costs[at, :] + y - u).astype(jnp.bfloat16)

                @pl.when(is_end)
                def _():
                    total[at, :] = u

            for copy in own_back:
                copy.start()
            v_ref[start, :] = jnp.zeros((BOUND, v_ref.shape[1]), jnp.bfloat16)

            @pl.loop(0, COUPLE // CHUNK)
            def _(c):
                at = pl.ds(pl.multiple_of(c * CHUNK, CHUNK), CHUNK)
                total[at, :] = jnp.zeros((CHUNK, total.shape[1]), jnp.float32)

        @pl.when(j == jnp.where(early, 0, 1))
        def _():
            fetch(r).wait()

        cut = pl.ds(pl.multiple_of(j * COUPLE, COUPLE), COUPLE)
        total[block(r), :] += product(matrix[block(r), cut], v_ref[cut, :])

        @pl.when((j == parts - 1) & early)
        def _():
            tail_back(r).start()

        @pl.when((j == parts - 1) & jnp.logical_not(early))
        def _():
            partial_back(r).start()

    @pl.loop(heads, 2 * heads)
    def _(r):
        tail_back(r).wait()

    for copy in own_back:
        copy.wait()

    @pl.loop(0, heads)
    def _(r):
        partial_back(r).wait()


def follow(matrix, costs, low, high, head, tail, v_own, v_new, u_start):
    size, width = costs.shape
    return pl.pallas_call(
        follow_kernel,
        out_shape=(f32(*tail.shape), bf16(*v_own.shape), f32(HEAD, width)),
        in_specs=[HBM, VMEM, VMEM, VMEM, HBM, HBM, HBM, VMEM, HBM],
        out_specs=(HBM,) * 3,
        input_output_aliases={5: 0, 6: 1},
        scratch_shapes=[
            pltpu.VMEM(matrix.shape, matrix.dtype),
            pltpu.VMEM((size, width), jnp.bfloat16),
            pltpu.VMEM((size, width), jnp.float32),
            pltpu.SemaphoreType.DMA((4, size // ROWS)),
        ],
        compiler_params=pltpu.CompilerParams(vmem_limit_bytes=24 * 1024 * 1024),
        cost_estimate=pl.CostEstimate(
            flops=2 * size * size * width, bytes_accessed=2 * size * size + 20 * HEAD * width, transcendentals=0
        ),
        name="follow",
    )(matrix, costs, low, high, head, tail, v_own, v_new, u_start)


def unwritten(*shape):
    return pl.pallas_call(lambda out: None, out_shape=f32(*shape), out_specs=HBM, name="unwritten")()


def transfers(couple, ends, colour, *rest):
    areas = lax.axis_size("area")
    windows = lax.axis_size("win")
    onward = [(i, i + 1) for i in range(windows - 1)]

    def swap(bits):
        def branch(c, e, *rest):
            if bits:
                other = lax.ppermute(c, "area", [(i, i ^ bits) for i in range(areas)])
            else:
                other = unwritten(*c.shape)
            return (other, lax.ppermute(e, "win", onward), *follow(*rest))

        return branch

    return lax.switch(colour, [swap(bits) for bits in range(areas)], couple, ends, *rest)


def finish_kernel(
    code, low, high, head_hbm, tail_hbm, other_hbm, before_hbm, z_out, u_out, total, joined, sems
):
    blocks, heads = total.shape[0] // ROWS, HEAD // ROWS
    at = lambda i: pl.ds(i * ROWS, ROWS)
    totals, joins = [], {}
    for i in range(blocks):
        source = head_hbm.at[at(i), :] if i < heads else tail_hbm.at[at(i - heads), :]
        totals.append(move(source, total.at[at(i), :], sems.at[0, i]))
        totals[i].start()
        if i < COUPLE // ROWS or i == heads:
            source = before_hbm if i == heads else other_hbm.at[at(i), :]
            joins[i] = move(source, joined.at[at(i), :], sems.at[1, i])
            joins[i].start()
    linked = (code[0] & (2**BITS - 1)) > 0
    out = []
    for i in range(blocks):
        rows = slice(i * ROWS, (i + 1) * ROWS)
        totals[i].wait()
        t = total[rows, :]
        z = clip(t, low[rows, :], high[rows, :])
        if i in joins:
            joins[i].wait()
            other = joined[rows, :]
            z = 0.5 * (z + other) if i == heads else jnp.where(linked, z + 0.5 * (other - z), z)
        joined[rows, :] = z
        total[rows, :] = t - z
        now = [
            move(joined.at[at(i), :], z_out.at[at(i), :], sems.at[2, i]),
            move(total.at[at(i), :], u_out.at[at(i), :], sems.at[3, i]),
        ]
        for copy in now:
            copy.start()
        out += now
    for copy in out:
        copy.wait()


def finish(code, low, high, head, tail, other, before):
    size, width = low.shape[0], head.shape[1]
    return pl.pallas_call(
        finish_kernel,
        out_shape=(f32(size, width), f32(size, width)),
        in_specs=[SMEM, VMEM, VMEM] + [HBM] * 4,
        out_specs=(HBM, HBM),
        scratch_shapes=[
            pltpu.VMEM((size, width), jnp.float32),
            pltpu.VMEM((size, width), jnp.float32),
            pltpu.SemaphoreType.DMA((4, size // ROWS)),
        ],
        name="finish",
    )(code, low, high, head, tail, other, before)


def local(kkt, offsets, lower, upper, partners, adjacency):
    matrix = kkt[0, 0]
    costs = offsets[0, 0]
    area = lax.axis_index("area")[None].astype(jnp.int32)
    code, words, low, high, v_own, partial, head, tail, before, other = prepare(
        area, partners, adjacency, lower[0], upper[0], matrix, costs
    )

    def iterate(carry):
        _, words, head, tail, v_own, partial, other, before = carry
        head, couple, ends, v_new, u_start, words, code, colour = lead(
            words, matrix, costs, low, high, head, tail, partial, other, before
        )
        other, before, tail, v_own, partial = transfers(
            couple, ends, colour[0], matrix, costs, low, high, head, tail, v_own, v_new, u_start
        )
        return code, words, head, tail, v_own, partial, other, before

    more = lambda carry: carry[0][0] >= 1 << (BITS + 1)
    carry = (code, words, head, tail, v_own, partial, other, before)
    code, _, head, tail, _, _, other, before = lax.while_loop(more, iterate, carry)
    z_now, u_now = finish(code, low, high, head, tail, other, before)
    return (z_now[None, None], u_now[None, None])


def solution(mesh):
    in_specs = (
        P("area", "win", None, None),
        P("area", "win", None, None),
        P("area", "win", None),
        P("area", "win", None),
        P(),
        P(),
    )
    out_specs = (P("area", "win", None, None), P("area", "win", None, None))
    return jax.shard_map(local, mesh=mesh, in_specs=in_specs, out_specs=out_specs, check_vma=False)
```
